32 devices in a mesh: grp: 8 (over z, x), lane: 4 (over y, core).
Axes of the slice: x: 2, y: 2, z: 4, core: 2. Of those that a mesh axis runs over, the one named last changes fastest.
Arguments:
- features: bfloat16 [65536, 128], P(('grp', 'lane')), may hold values from -600 to 600
- tiles: bfloat16 [512, 7, 128, 128], P(('grp', 'lane')), may hold values from -0.125 to 0.125
- tile_cols: int32 [512, 7], P(('grp', 'lane')), may hold values from 0 to 23
- send_index: int32 [32, 2, 512], P(('grp', 'lane')), may hold values from 0 to 2047
- send_count: int32 [32, 2], P(('grp', 'lane')), may hold values from 128 to 512, as said below
- coef: float32 [4, 128], replicated, may hold values from -1 to 1
- dest_lane: int32 [65536], P(('grp', 'lane')), may hold values from 0 to 3, as said below
- dest_slot: int32 [65536], P(('grp', 'lane')), may hold values from 0 to 2047, as said below
Outputs:
- table_out: bfloat16 [65536, 128], P(('grp', 'lane'))
The draws below stay inside these ranges and needn't reach their ends.
Inputs may be any that keep to these rules, and one draw needn't show every extreme that they name: `send_count`: in every draw for each of the two directions some partition has exactly 512 live rows towards that neighbour. `dest_lane`: within each relayout group every row of every table shard is named by exactly one node; at most 1024 rows of one partition go to one shard, and exactly 1024 for some pair in every group. `dest_slot`: together with dest_lane, a one-to-one map of a group's nodes onto its table rows.
All inputs are finite; a program needn't handle non-finite values.
Results may differ from the reference program's by a relative error of at most 0.008.
Values may be sent and summed in bfloat16 or wider, within the bound.
A program may use at most 64 MiB of HBM per device.

```python
import math
import jax
import jax.numpy as jnp
from jax import lax

F = 128
TILE = 128
KT = 7
ORDER = 3
ROWS = 2048
BND = 512
NODES = 65536
N_GRP = 8
N_LANE = 4
DEVICES = 32


def draw_features(key, part):
    first_key, second_key, third_key = jax.random.split(key, 3)
    position = jnp.arange(NODES).astype(jnp.float32)[:, None] / NODES
    row_scale = jnp.exp(jax.random.uniform(second_key, (NODES, 1)) * math.log(10.0))
    col_scale = jnp.exp(jax.random.uniform(third_key, (1, F)) * math.log(10.0))
    values = jnp.clip(jax.random.normal(first_key, (NODES, F)), -6.0, 6.0)
    ramp = 1.0 + 2.0 * position
    return (values * row_scale * col_scale * ramp / 10.0).astype(jnp.bfloat16)


def draw_send_count(key, part):
    first_key, second_key = jax.random.split(jax.random.fold_in(key, 11), 2)
    counts = jax.random.randint(first_key, (DEVICES, 2), BND // 4, BND + 1)
    fullest = jax.random.randint(second_key, (2,), 0, DEVICES)
    counts = counts.at[fullest[0], 0].set(BND)
    counts = counts.at[fullest[1], 1].set(BND)
    return counts.astype(jnp.int32)


def relay_plan(key):
    base_key = jax.random.fold_in(key, 77)
    mean_load = ROWS // N_LANE
    lane_ids = jnp.arange(N_LANE)
    lane_load = jnp.where(lane_ids == 0, 2 * mean_load, jnp.where((lane_ids == 1) | (lane_ids == 2), mean_load // 2, mean_load))
    rotation = jax.random.randint(jax.random.fold_in(base_key, 1), (N_GRP,), 0, N_LANE)
    counts = lane_load[(lane_ids[None, None, :] - lane_ids[None, :, None] + rotation[:, None, None]) % N_LANE]
    run_ends = jnp.cumsum(counts, axis=2)
    run_starts = run_ends - counts
    position = jnp.arange(ROWS)
    sorted_dest = jnp.sum((position[None, None, :, None] >= run_ends[:, :, None, :]).astype(jnp.int32), axis=3)
    rank_in_run = position[None, None, :] - jnp.take_along_axis(run_starts, sorted_dest, axis=2)
    offsets = jnp.cumsum(counts, axis=1) - counts
    placement = jnp.take_along_axis(offsets, sorted_dest, axis=2) + rank_in_run
    row_keys = jax.random.split(jax.random.fold_in(base_key, 2), N_GRP * N_LANE)
    shuffle = jax.vmap(lambda k: jax.random.permutation(k, ROWS))(row_keys).reshape(N_GRP, N_LANE, ROWS)
    destination = jnp.take_along_axis(sorted_dest, shuffle, axis=2)
    place_rows = jnp.take_along_axis(placement, shuffle, axis=2)
    slot_keys = jax.random.split(jax.random.fold_in(base_key, 3), N_GRP * N_LANE)
    slot_perm = jax.vmap(lambda k: jax.random.permutation(k, ROWS))(slot_keys).reshape(N_GRP, N_LANE, ROWS)
    group_ids = jnp.arange(N_GRP)[:, None, None]
    slot_ids = slot_perm[group_ids, destination, place_rows]
    return (destination.reshape(-1).astype(jnp.int32), slot_ids.reshape(-1).astype(jnp.int32))


def draw_dest_lane(key, part):
    return relay_plan(key)[0]


def draw_dest_slot(key, part):
    return relay_plan(key)[1]


def plant(array, stream_key, low, high):
    longest = array.shape.index(max(array.shape))
    spots = []
    for shift in (0, 1):
        where = [jax.random.randint(jax.random.fold_in(stream_key, axis), (), 0, length) for axis, length in enumerate(array.shape)]
        where[longest] = (where[longest] + shift) % array.shape[longest]
        spots.append(tuple(where))
    return array.at[spots[0]].set(low).at[spots[1]].set(high)


def block_scale(stream_key, extent, shards, least, top_value):
    level, own = 1.0, jax.random.fold_in(stream_key, 6)
    for dim, blocks in shards:
        heights = jnp.exp(jax.random.uniform(jax.random.fold_in(own, dim), (blocks,), jnp.float32, least / len(shards), top_value / len(shards)))
        level = level * jnp.repeat(heights, extent[dim] // blocks).reshape([-1 if axis == dim else 1 for axis in range(len(extent))])
    return level


def centred(own_key, dims, scale, bound, pieces=(), dtype=jnp.bfloat16):
    array = jax.random.normal(own_key, dims, jnp.float32) * scale
    if len(pieces) > 0:
        array = block_scale(own_key, dims, pieces, -0.22, 0.18) * array
    return jnp.clip(array, min=-bound, max=bound).astype(dtype)


def setup_inputs(seed: int = 0) -> dict:
    keys = jax.random.split(jax.random.key(seed), 9)
    features = draw_features(jax.random.fold_in(keys[8], 71), 0)
    tiles = centred(keys[1], (NODES // TILE, KT, TILE, TILE), (2 * KT * TILE) ** -0.5, 0.125, ((0, 32),))
    tile_cols = plant(jax.random.randint(keys[2], (NODES // TILE, KT), 0, ROWS // TILE + 2 * BND // TILE), jax.random.fold_in(keys[2], 1), 0, (ROWS // TILE + 2 * BND // TILE) - 1).astype(jnp.int32)
    send_index = plant(jax.random.randint(keys[3], (DEVICES, 2, BND), 0, ROWS), jax.random.fold_in(keys[3], 1), 0, ROWS - 1).astype(jnp.int32)
    send_count = draw_send_count(jax.random.fold_in(keys[8], 71), 0)
    coef = jnp.clip(jax.random.uniform(keys[5], (ORDER + 1, F), jnp.float32, -1.0, 1.0), -1.0, 1.0)
    dest_lane = draw_dest_lane(jax.random.fold_in(keys[8], 71), 0)
    dest_slot = draw_dest_slot(jax.random.fold_in(keys[8], 71), 0)
    return {"features": features, "tiles": tiles, "tile_cols": tile_cols, "send_index": send_index, "send_count": send_count, "coef": coef, "dest_lane": dest_lane, "dest_slot": dest_slot}


def operate_all(current, tile_set, column_ids, index_set, valid_rows):
    picked = jax.vmap(jax.vmap(lambda c, i: c[i]))(current, index_set)
    picked = jnp.where(valid_rows[..., None], picked, jnp.zeros_like(picked))
    from_lower = jnp.roll(picked[:, :, 0], 1, axis=0)
    from_upper = jnp.roll(picked[:, :, 1], -1, axis=0)
    extended = jnp.concatenate([current, from_lower, from_upper], axis=2)
    extended = extended.reshape(N_GRP, N_LANE, -1, TILE, F)

    def per_group(packed):
        group_ext, group_tiles, group_cols = packed

        def per_device(dev_ext, dev_tiles, dev_cols):
            blocks = dev_ext[dev_cols].astype(jnp.float32)
            result = jnp.einsum('bkij,bkjf->bif', dev_tiles.astype(jnp.float32), blocks)
            return result.reshape(ROWS, F)
        return jax.vmap(per_device)(group_ext, group_tiles, group_cols)
    return lax.map(per_group, (extended, tile_set, column_ids))

def reference(features, tiles, tile_cols, send_index, send_count, coef, dest_lane, dest_slot):
    blocks_dev = ROWS // TILE
    tile_set = tiles.reshape(N_GRP, N_LANE, blocks_dev, KT, TILE, TILE)
    column_ids = tile_cols.reshape(N_GRP, N_LANE, blocks_dev, KT)
    index_set = send_index.reshape(N_GRP, N_LANE, 2, BND)
    counts = send_count.reshape(N_GRP, N_LANE, 2)
    valid_rows = jnp.arange(BND).astype(jnp.int32)[None, None, None, :] < counts[..., None]
    cheb_terms = [features.reshape(N_GRP, N_LANE, ROWS, F)]
    first = operate_all(cheb_terms[0], tile_set, column_ids, index_set, valid_rows)
    cheb_terms.append(first.astype(jnp.bfloat16))
    for term_order in range(2, ORDER + 1):
        applied = operate_all(cheb_terms[-1], tile_set, column_ids, index_set, valid_rows)
        nxt = 2.0 * applied - cheb_terms[-2].astype(jnp.float32)
        cheb_terms.append(nxt.astype(jnp.bfloat16))
    mixed = jnp.zeros((NODES, F), jnp.float32)
    for term_order in range(ORDER + 1):
        mixed = mixed + coef[term_order][None, :] * cheb_terms[term_order].reshape(NODES, F).astype(jnp.float32)
    gram = jnp.dot(mixed.T, mixed, precision=lax.Precision.HIGHEST)
    factor = jnp.linalg.cholesky(gram)
    white = jax.scipy.linalg.solve_triangular(factor, mixed.T, lower=True).T * jnp.sqrt(jnp.float32(NODES))
    norms = jnp.sqrt(lax.optimization_barrier(jnp.sum(white * white, axis=1, keepdims=True)) + 1e-06)
    radius = jnp.sqrt(jnp.float32(F))
    ball_rows = (jnp.tanh(norms / radius) * radius * white / norms).astype(jnp.bfloat16)
    group_of = jnp.arange(NODES).astype(jnp.int32) // (N_LANE * ROWS)
    target = (group_of * N_LANE + dest_lane) * ROWS + dest_slot
    table_out = jnp.zeros((NODES, F), jnp.bfloat16).at[target].set(ball_rows)
    return table_out
```

```python
import functools
import math

import jax
import jax.numpy as jnp
from jax import lax
from jax.experimental import pallas as pl
from jax.experimental.pallas import tpu as pltpu
from jax.sharding import PartitionSpec as P

MESH = pl.DeviceIdType.MESH
BF = jnp.bfloat16
F32 = jnp.float32
ORDER = 3
SUB = 8


def onehot(flags):
    return jnp.where(flags, 1.0, 0.0).astype(BF)


def eliminate(gram, node_total):
    size = gram.shape[0]
    blocks = size // SUB
    sub = lax.broadcasted_iota(jnp.int32, (SUB, size), 0)
    lane = lax.broadcasted_iota(jnp.int32, (SUB, size), 1)
    left = [gram[i * SUB : (i + 1) * SUB, :] for i in range(blocks)]
    right = [jnp.where(lane == sub + i * SUB, 1.0, 0.0).astype(F32) for i in range(blocks)]
    for j in range(size):
        own, row = divmod(j, SUB)
        pivot_row = left[own][row : row + 1, :]
        pivot_right = right[own][row : row + 1, :]
        inverse = 1.0 / pivot_row[:, j : j + 1]
        scaled = pivot_row * inverse
        scaled_right = pivot_right * inverse
        for i in range(own, blocks):
            column = left[i][:, j : j + 1]
            if i == own:
                column = jnp.where(sub[:, :1] > row, column, 0.0)
            left[i] = left[i] - column * scaled
            right[i] = right[i] - column * scaled_right
    root = math.sqrt(node_total)
    result = []
    for i in range(blocks):
        pivots = jnp.sum(jnp.where(lane == sub + i * SUB, left[i], 0.0), axis=1, keepdims=True)
        result.append(right[i] * (root / jnp.sqrt(pivots)))
    return jnp.concatenate(result, axis=0)


def kernel(
    groups, lanes, cols, counts, feats, tiles, index, coef, dest_lane, dest_slot, out,
    ext0, ext1, ext2, tile_v, pick, snd, mixed, low, gat, codes, part, rs_buf, lane_buf, chunk, tot, placed,
    load_sem, halo_s, halo_r, code_s, code_r, rs_s, rs_r, ln_s, ln_r, ag_s, ag_r, x_s, x_r, f_s, f_r,
):
    g, l = lax.axis_index("grp"), lax.axis_index("lane")
    own_blocks, tile, width = feats.shape
    rows = own_blocks * tile
    ext = (ext0, ext1, ext2)
    per_block = tiles.shape[1]
    bnd = index.shape[1]
    lists = bnd // tile
    node_total = rows * groups * lanes
    half = lanes // 2
    sibling = l + 1 - 2 * lax.rem(l, 2)

    def grp_at(t):
        return (lax.rem(g + t + groups, groups), l)

    def lane_at(t):
        return (g, lax.rem(l + t + lanes, lanes))

    load_tiles = pltpu.make_async_copy(tiles, tile_v, load_sem.at[0])
    load_feats = pltpu.make_async_copy(feats, ext[0].at[pl.ds(0, own_blocks)], load_sem.at[1])
    load_feats.start()
    load_tiles.start()

    barrier = pltpu.get_barrier_semaphore()
    for t in range(1, groups):
        pl.semaphore_signal(barrier, inc=1, device_id=grp_at(t), device_id_type=MESH)
    for t in range(1, lanes):
        pl.semaphore_signal(barrier, inc=1, device_id=lane_at(t), device_id_type=MESH)

    codes[0] = dest_lane[...] * rows + dest_slot[...]

    row_pos = lax.broadcasted_iota(jnp.int32, (tile, tile), 0)
    lane_pos = lax.broadcasted_iota(jnp.int32, (tile, tile), 1)
    for d in range(2):
        for c in range(bnd // tile):
            wanted = jnp.broadcast_to(index[d : d + 1, c * tile : (c + 1) * tile], (tile, tile)).T
            wanted = jnp.where(row_pos + c * tile < counts[0, d], wanted, -1)
            for r in range(rows // tile):
                pick[pl.ds(d * bnd + c * tile, tile), pl.ds(r * tile, tile)] = onehot(
                    wanted == lane_pos + r * tile
                )

    load_feats.wait()
    pl.semaphore_wait(barrier, groups - 1 + lanes - 1)

    def remote(src, dst, s, r, device):
        return pltpu.make_async_remote_copy(
            src_ref=src, dst_ref=dst, send_sem=s, recv_sem=r, device_id=device, device_id_type=MESH
        )

    def halo(k):
        copies = []
        for d in range(2):
            def gather(c, _, d=d):
                at = pl.multiple_of(d * bnd + c * 256, 256)
                picked = jnp.dot(
                    pick[pl.ds(at, 256), :], ext[k][pl.ds(0, own_blocks)].reshape(rows, width),
                    preferred_element_type=F32
                ).astype(BF)
                for part_at in range(256 // tile):
                    snd[k, (d * bnd + c * 256) // tile + part_at] = picked[
                        part_at * tile : (part_at + 1) * tile
                    ]
                return 0
            lax.fori_loop(0, bnd // 256, gather, 0)
            copy = remote(
                snd.at[k, pl.ds(d * lists, lists)], ext[k].at[pl.ds(own_blocks + d * lists, lists)],
                halo_s.at[k, d], halo_r.at[k, d], grp_at(1 - 2 * d),
            )
            copy.start()
            copies.append(copy)
        return copies

    halo_copies = halo(0)
    code_copies = []
    for t in range(1, lanes):
        copy = remote(codes.at[0], codes.at[t], code_s.at[t], code_r.at[t], lane_at(t))
        copy.start()
        code_copies.append(copy)
    load_tiles.wait()

    for k in range(1, ORDER + 1):
        for copy in halo_copies:
            copy.wait()

        def block(b, _, k=k):
            at = pl.ds(pl.multiple_of(b * tile, tile), tile)
            lhs = jnp.concatenate([tile_v[b, j] for j in range(per_block)], axis=1)
            rhs = jnp.concatenate(
                [
                    ext[k - 1][cols[b, j]]
                    for j in range(per_block)
                ],
                axis=0,
            )
            value = jnp.dot(lhs, rhs, preferred_element_type=F32)
            if k > 1:
                value = 2.0 * value - ext[k - 2][b].astype(F32)
            term = value.astype(BF)
            if k == 1:
                total = coef[0:1, :] * ext[0][b].astype(F32)
            else:
                total = mixed[at]
            total = total + coef[k : k + 1, :] * term.astype(F32)
            if k < ORDER:
                ext[k][b] = term
                mixed[at] = total
            else:
                high = total.astype(BF)
                gat[0, at] = high
                low[at] = (total - high.astype(F32)).astype(BF)
            return 0

        lax.fori_loop(0, rows // tile, block, 0, unroll=4)
        if k < ORDER:
            halo_copies = halo(k)

    step = 512
    square = jnp.zeros((2 * width, 2 * width), F32)
    for c in range(rows // step):
        both = jnp.concatenate([gat[0, pl.ds(c * step, step)], low[pl.ds(c * step, step)]], axis=1)
        square = square + lax.dot_general(
            both, both, (((0,), (0,)), ((), ())), preferred_element_type=F32
        )
    own_gram = (square[:width, :width] + square[width:, width:]) + (
        square[:width, width:] + square[width:, :width]
    )
    share = width // groups
    for t in range(groups):
        part[t] = own_gram[t * share : (t + 1) * share, :]

    rs_copies = []
    for t in range(1, groups):
        peer = grp_at(t)
        copy = remote(part.at[peer[0]], rs_buf.at[t], rs_s.at[t], rs_r.at[t], peer)
        copy.start()
        rs_copies.append(copy)
    sib_copies = [remote(gat.at[0], gat.at[half], f_s.at[0], f_r.at[0], (g, sibling))]
    sib_copies[0].start()
    for copy in code_copies:
        copy.wait()

    def place(gat_slot, code_slot, first):
        tall = 256

        def body(c, _):
            at = pl.ds(pl.multiple_of(c * tall, tall), tall)
            target = lax.broadcasted_iota(jnp.int32, (tall, tile), 0) + (c * tall + l * rows)
            selector = jnp.concatenate(
                [onehot(codes[code_slot, r : r + 1, :] == target) for r in range(rows // tile)], axis=1
            )
            value = jnp.dot(selector, gat[gat_slot], preferred_element_type=F32).astype(BF)
            if first:
                placed[at] = value
            else:
                placed[at] = placed[at] + value
            return 0

        lax.fori_loop(0, rows // tall, body, 0)

    for copy in rs_copies:
        copy.wait()
    summed = part[g]
    for t in range(1, groups):
        summed = summed + rs_buf[t]
    lane_buf[0] = summed
    ln_copies = []
    for t in range(1, lanes):
        copy = remote(lane_buf.at[0], lane_buf.at[t], ln_s.at[t], ln_r.at[t], lane_at(t))
        copy.start()
        ln_copies.append(copy)
    x_copies = [None]
    for t in range(1, half):
        copy = remote(gat.at[0], gat.at[t], x_s.at[t], x_r.at[t], lane_at(2 * t))
        copy.start()
        x_copies.append(copy)
    for copy in ln_copies:
        copy.wait()
    total_chunk = lane_buf[0]
    for t in range(1, lanes):
        total_chunk = total_chunk + lane_buf[t]
    chunk[...] = total_chunk
    tot[0] = total_chunk
    ag_copies = []
    for t in range(1, groups):
        copy = remote(chunk, tot.at[t], ag_s.at[t], ag_r.at[t], grp_at(t))
        copy.start()
        ag_copies.append(copy)
    place(0, 0, True)
    for copy in ag_copies:
        copy.wait()
    gram = jnp.concatenate(
        [tot[lax.rem(g - r + groups, groups)] for r in range(groups)], axis=0
    )
    whitener = eliminate(gram, node_total)
    high = whitener.astype(BF)
    rhs = jnp.concatenate([high, (whitener - high.astype(F32)).astype(BF)], axis=0)

    for t in range(1, half):
        x_copies[t].wait()
        copy = remote(gat.at[t], gat.at[half + t], f_s.at[t], f_r.at[t], (g, sibling))
        copy.start()
        sib_copies.append(copy)
    for t in range(1, half):
        place(t, 2 * t, False)
    for t in range(half):
        sib_copies[t].wait()
        place(half + t, lax.rem(l - sibling + 2 * t + lanes, lanes), False)

    radius = math.sqrt(width)

    def ball(c, _):
        at = pl.ds(pl.multiple_of(c * 256, 256), 256)
        pair = lax.dot_general(
            placed[at], rhs, (((1,), (1,)), ((), ())), preferred_element_type=F32
        )
        white = pair[:, :width] + pair[:, width:]
        norms = jnp.sqrt(jnp.sum(white * white, axis=1, keepdims=True) + 1e-06)
        out[at] = (white * (jnp.tanh(norms / radius) * radius / norms)).astype(BF)
        return 0

    lax.fori_loop(0, rows // 256, ball, 0)


def body(features, tiles, tile_cols, send_index, send_count, coef, dest_lane, dest_slot):
    groups, lanes = lax.axis_size("grp"), lax.axis_size("lane")
    rows, width = features.shape
    blocks, per_block, tile, _ = tiles.shape
    bnd = send_index.shape[2]
    half = lanes // 2
    share = width // groups
    dma = pltpu.SemaphoreType.DMA
    vmem = pl.BlockSpec(memory_space=pltpu.VMEM)
    smem = pl.BlockSpec(memory_space=pltpu.SMEM)
    hbm = pl.BlockSpec(memory_space=pl.ANY)
    return pl.pallas_call(
        functools.partial(kernel, groups, lanes),
        out_shape=jax.ShapeDtypeStruct((rows, width), BF),
        in_specs=[smem, smem, hbm, hbm, vmem, vmem, vmem, vmem],
        out_specs=vmem,
        scratch_shapes=[
            *[pltpu.VMEM(((rows + 2 * bnd) // tile, tile, width), BF)] * ORDER,
            pltpu.VMEM((blocks, per_block, tile, tile), BF),
            pltpu.VMEM((2 * bnd, rows), BF),
            pltpu.VMEM((ORDER, 2 * bnd // tile, tile, width), BF),
            pltpu.VMEM((rows, width), F32),
            pltpu.VMEM((rows, width), BF),
            pltpu.VMEM((lanes, rows, width), BF),
            pltpu.VMEM((lanes, rows // 128, 128), jnp.int32),
            pltpu.VMEM((groups, share, width), F32),
            pltpu.VMEM((groups, share, width), F32),
            pltpu.VMEM((lanes, share, width), F32),
            pltpu.VMEM((share, width), F32),
            pltpu.VMEM((groups, share, width), F32),
            pltpu.VMEM((rows, width), BF),
            dma((2,)),
            dma((ORDER, 2)), dma((ORDER, 2)),
            dma((lanes,)), dma((lanes,)),
            dma((groups,)), dma((groups,)),
            dma((lanes,)), dma((lanes,)),
            dma((groups,)), dma((groups,)),
            dma((half,)), dma((half,)),
            dma((half,)), dma((half,)),
        ],
        compiler_params=pltpu.CompilerParams(
            collective_id=0, has_side_effects=True, vmem_limit_bytes=52 * 1024 * 1024
        ),
    )(
        tile_cols, send_count, features.reshape(-1, tile, width), tiles, send_index.reshape(2, bnd), coef,
        dest_lane.reshape(-1, 128), dest_slot.reshape(-1, 128),
    )


def solution(mesh):
    placed = (
        P(("grp", "lane"), None),
        P(("grp", "lane"), None, None, None),
        P(("grp", "lane"), None),
        P(("grp", "lane"), None, None),
        P(("grp", "lane"), None),
        P(),
        P(("grp", "lane")),
        P(("grp", "lane")),
    )
    return jax.shard_map(
        body, mesh=mesh, in_specs=placed, out_specs=P(("grp", "lane"), None), check_vma=False
    )
```

```python
import functools
import math

import jax
import jax.numpy as jnp
from jax import lax
from jax.experimental import pallas as pl
from jax.experimental.pallas import tpu as pltpu
from jax.sharding import PartitionSpec as P

MESH = pl.DeviceIdType.MESH
BF = jnp.bfloat16
F32 = jnp.float32
ORDER = 3
SUB = 8


def onehot(flags):
    return jnp.where(flags, 1.0, 0.0).astype(BF)


def eliminate(gram, node_total):
    size = gram.shape[0]
    blocks = size // SUB
    sub = lax.broadcasted_iota(jnp.int32, (SUB, size), 0)
    lane = lax.broadcasted_iota(jnp.int32, (SUB, size), 1)
    left = [gram[i * SUB : (i + 1) * SUB, :] for i in range(blocks)]
    right = [jnp.where(lane == sub + i * SUB, 1.0, 0.0).astype(F32) for i in range(blocks)]
    for j in range(size):
        own, row = divmod(j, SUB)
        pivot_row = left[own][row : row + 1, :]
        pivot_right = right[own][row : row + 1, :]
        inverse = 1.0 / pivot_row[:, j : j + 1]
        scaled = pivot_row * inverse
        scaled_right = pivot_right * inverse
        for i in range(own, blocks):
            column = left[i][:, j : j + 1]
            if i == own:
                column = jnp.where(sub[:, :1] > row, column, 0.0)
            left[i] = left[i] - column * scaled
            right[i] = right[i] - column * scaled_right
    root = math.sqrt(node_total)
    result = []
    for i in range(blocks):
        pivots = jnp.sum(jnp.where(lane == sub + i * SUB, left[i], 0.0), axis=1, keepdims=True)
        result.append(right[i] * (root / jnp.sqrt(pivots)))
    return jnp.concatenate(result, axis=0)


def kernel(
    groups, lanes, cols_h, counts_h, feats, tiles, index_h, coef_h, dest_lane_h, dest_slot_h, out,
    cols, counts, index, coef, dest_lane, dest_slot, ready,
    ext0, ext1, ext2, tile_v, pick, snd, mixed, low, gat, codes, part, rs_buf, lane_buf, chunk, tot, placed,
    load_sem, halo_s, halo_r, code_s, code_r, rs_s, rs_r, ln_s, ln_r, ag_s, ag_r, x_s, x_r, f_s, f_r,
):
    g, l = lax.axis_index("grp"), lax.axis_index("lane")
    own_blocks, tile, width = feats.shape
    rows = own_blocks * tile
    ext = (ext0, ext1, ext2)
    per_block = tiles.shape[1]
    bnd = index_h.shape[1]
    lists = bnd // tile
    node_total = rows * groups * lanes
    half = lanes // 2
    sibling = l + 1 - 2 * lax.rem(l, 2)

    def grp_at(t):
        return (lax.rem(g + t + groups, groups), l)

    def lane_at(t):
        return (g, lax.rem(l + t + lanes, lanes))

    load_tiles = pltpu.make_async_copy(tiles, tile_v, load_sem.at[0])
    load_feats = pltpu.make_async_copy(feats, ext[0].at[pl.ds(0, own_blocks)], load_sem.at[1])
    small = [
        pltpu.make_async_copy(src, dst, load_sem.at[2 + i])
        for i, (src, dst) in enumerate(
            [
                (index_h, index), (counts_h, counts), (dest_lane_h, dest_lane),
                (dest_slot_h, dest_slot), (cols_h, cols), (coef_h, coef),
            ]
        )
    ]
    for copy in small[:4]:
        copy.start()
    load_feats.start()
    load_tiles.start()
    for copy in small[4:]:
        copy.start()

    barrier = pltpu.get_barrier_semaphore()
    for t in range(1, groups):
        pl.semaphore_signal(barrier, inc=1, device_id=grp_at(t), device_id_type=MESH)
    for t in range(1, lanes):
        pl.semaphore_signal(barrier, inc=1, device_id=lane_at(t), device_id_type=MESH)

    for copy in small[:4]:
        copy.wait()
    codes[0] = dest_lane[...] * rows + dest_slot[...]

    row_pos = lax.broadcasted_iota(jnp.int32, (tile, tile), 0)
    lane_pos = lax.broadcasted_iota(jnp.int32, (tile, tile), 1)
    for d in range(2):
        for c in range(bnd // tile):
            wanted = jnp.broadcast_to(index[d : d + 1, c * tile : (c + 1) * tile], (tile, tile)).T
            wanted = jnp.where(row_pos + c * tile < counts[0, d], wanted, -1)
            for r in range(rows // tile):
                pick[pl.ds(d * bnd + c * tile, tile), pl.ds(r * tile, tile)] = onehot(
                    wanted == lane_pos + r * tile
                )

    load_feats.wait()
    pl.semaphore_wait(barrier, groups - 1 + lanes - 1)

    def remote(src, dst, s, r, device):
        return pltpu.make_async_remote_copy(
            src_ref=src, dst_ref=dst, send_sem=s, recv_sem=r, device_id=device, device_id_type=MESH
        )

    def halo(k):
        copies = []
        for d in range(2):
            def gather(c, _, d=d):
                at = pl.multiple_of(d * bnd + c * 256, 256)
                picked = jnp.dot(
                    pick[pl.ds(at, 256), :], ext[k][pl.ds(0, own_blocks)].reshape(rows, width),
                    preferred_element_type=F32
                ).astype(BF)
                for part_at in range(256 // tile):
                    snd[k, (d * bnd + c * 256) // tile + part_at] = picked[
                        part_at * tile : (part_at + 1) * tile
                    ]
                return 0
            lax.fori_loop(0, bnd // 256, gather, 0)
            copy = remote(
                snd.at[k, pl.ds(d * lists, lists)], ext[k].at[pl.ds(own_blocks + d * lists, lists)],
                halo_s.at[k, d], halo_r.at[k, d], grp_at(1 - 2 * d),
            )
            copy.start()
            copies.append(copy)
        return copies

    tall = 256

    def selector(code_slot, c):
        target = lax.broadcasted_iota(jnp.int32, (tall, tile), 0) + (c * tall + l * rows)
        return jnp.concatenate(
            [onehot(codes[code_slot, r : r + 1, :] == target) for r in range(rows // tile)], axis=1
        )

    def prepare(code_slot, slot):
        def step(c, _):
            ready[slot, pl.ds(pl.multiple_of(c * tall, tall), tall)] = selector(code_slot, c)
            return 0

        lax.fori_loop(0, rows // tall, step, 0)

    def place(gat_slot, code_slot, first=False, slot=None):
        def step(c, _):
            at = pl.ds(pl.multiple_of(c * tall, tall), tall)
            chosen = selector(code_slot, c) if slot is None else ready[slot, at]
            value = jnp.dot(chosen, gat[gat_slot], preferred_element_type=F32).astype(BF)
            placed[at] = value if first else placed[at] + value
            return 0

        lax.fori_loop(0, rows // tall, step, 0)

    def passed_code(t):
        return lax.rem(l - sibling + 2 * t + lanes, lanes)

    halo_copies = halo(0)
    code_copies = []
    for t in range(1, lanes):
        copy = remote(codes.at[0], codes.at[t], code_s.at[t], code_r.at[t], lane_at(t))
        copy.start()
        code_copies.append(copy)
    load_tiles.wait()
    for copy in small[4:]:
        copy.wait()

    for k in range(1, ORDER + 1):
        for copy in halo_copies:
            copy.wait()

        def block(b, _, k=k):
            at = pl.ds(pl.multiple_of(b * tile, tile), tile)
            lhs = jnp.concatenate([tile_v[b, j] for j in range(per_block)], axis=1)
            rhs = jnp.concatenate(
                [
                    ext[k - 1][cols[b, j]]
                    for j in range(per_block)
                ],
                axis=0,
            )
            value = jnp.dot(lhs, rhs, preferred_element_type=F32)
            if k > 1:
                value = 2.0 * value - ext[k - 2][b].astype(F32)
            term = value.astype(BF)
            if k == 1:
                total = coef[0:1, :] * ext[0][b].astype(F32)
            else:
                total = mixed[at]
            total = total + coef[k : k + 1, :] * term.astype(F32)
            if k < ORDER:
                ext[k][b] = term
                mixed[at] = total
            else:
                high = total.astype(BF)
                gat[0, at] = high
                low[at] = (total - high.astype(F32)).astype(BF)
            return 0

        lax.fori_loop(0, rows // tile, block, 0, unroll=4)
        if k < ORDER:
            halo_copies = halo(k)
            if k == 1:
                for copy in code_copies:
                    copy.wait()
                if half > 1:
                    prepare(2, 0)
            elif k == 2 and half > 1:
                prepare(passed_code(1), 1)

    step = 512
    square = jnp.zeros((2 * width, 2 * width), F32)
    for c in range(rows // step):
        both = jnp.concatenate([gat[0, pl.ds(c * step, step)], low[pl.ds(c * step, step)]], axis=1)
        square = square + lax.dot_general(
            both, both, (((0,), (0,)), ((), ())), preferred_element_type=F32
        )
    own_gram = (square[:width, :width] + square[width:, width:]) + (
        square[:width, width:] + square[width:, :width]
    )
    share = width // groups
    for t in range(groups):
        part[t] = own_gram[t * share : (t + 1) * share, :]

    rs_copies = []
    for t in range(1, groups):
        peer = grp_at(t)
        copy = remote(part.at[peer[0]], rs_buf.at[t], rs_s.at[t], rs_r.at[t], peer)
        copy.start()
        rs_copies.append(copy)
    sib_copies = [remote(gat.at[0], gat.at[half], f_s.at[0], f_r.at[0], (g, sibling))]
    sib_copies[0].start()
    place(0, 0, first=True)

    for copy in rs_copies:
        copy.wait()
    summed = part[g]
    for t in range(1, groups):
        summed = summed + rs_buf[t]
    lane_buf[0] = summed
    ln_copies = []
    for t in range(1, lanes):
        copy = remote(lane_buf.at[0], lane_buf.at[t], ln_s.at[t], ln_r.at[t], lane_at(t))
        copy.start()
        ln_copies.append(copy)
    x_copies = [None]
    for t in range(1, half):
        copy = remote(gat.at[0], gat.at[t], x_s.at[t], x_r.at[t], lane_at(2 * t))
        copy.start()
        x_copies.append(copy)
    for copy in ln_copies:
        copy.wait()
    total_chunk = lane_buf[0]
    for t in range(1, lanes):
        total_chunk = total_chunk + lane_buf[t]
    chunk[...] = total_chunk
    tot[0] = total_chunk
    ag_copies = []
    for t in range(1, groups):
        copy = remote(chunk, tot.at[t], ag_s.at[t], ag_r.at[t], grp_at(t))
        copy.start()
        ag_copies.append(copy)
    sib_copies[0].wait()
    place(half, passed_code(0))
    for copy in ag_copies:
        copy.wait()
    gram = jnp.concatenate(
        [tot[lax.rem(g - r + groups, groups)] for r in range(groups)], axis=0
    )
    whitener = eliminate(gram, node_total)
    high = whitener.astype(BF)
    rhs = jnp.concatenate([high, (whitener - high.astype(F32)).astype(BF)], axis=0)

    for t in range(1, half):
        x_copies[t].wait()
        copy = remote(gat.at[t], gat.at[half + t], f_s.at[t], f_r.at[t], (g, sibling))
        copy.start()
        sib_copies.append(copy)
    for t in range(1, half):
        place(t, 2 * t, slot=0 if t == 1 else None)
    for t in range(1, half):
        sib_copies[t].wait()
        place(half + t, passed_code(t), slot=1 if t == 1 else None)

    radius = math.sqrt(width)

    def ball(c, _):
        at = pl.ds(pl.multiple_of(c * 256, 256), 256)
        pair = lax.dot_general(
            placed[at], rhs, (((1,), (1,)), ((), ())), preferred_element_type=F32
        )
        white = pair[:, :width] + pair[:, width:]
        norms = jnp.sqrt(jnp.sum(white * white, axis=1, keepdims=True) + 1e-06)
        out[at] = (white * (jnp.tanh(norms / radius) * radius / norms)).astype(BF)
        return 0

    lax.fori_loop(0, rows // 256, ball, 0)


def body(features, tiles, tile_cols, send_index, send_count, coef, dest_lane, dest_slot):
    groups, lanes = lax.axis_size("grp"), lax.axis_size("lane")
    rows, width = features.shape
    blocks, per_block, tile, _ = tiles.shape
    bnd = send_index.shape[2]
    half = lanes // 2
    share = width // groups
    dma = pltpu.SemaphoreType.DMA
    vmem = pl.BlockSpec(memory_space=pltpu.VMEM)
    hbm = pl.BlockSpec(memory_space=pl.ANY)
    return pl.pallas_call(
        functools.partial(kernel, groups, lanes),
        out_shape=jax.ShapeDtypeStruct((rows, width), BF),
        in_specs=[hbm] * 8,
        out_specs=vmem,
        scratch_shapes=[
            pltpu.SMEM((blocks, per_block), jnp.int32),
            pltpu.SMEM((1, 2), jnp.int32),
            pltpu.VMEM((2, bnd), jnp.int32),
            pltpu.VMEM((ORDER + 1, width), F32),
            pltpu.VMEM((rows // 128, 128), jnp.int32),
            pltpu.VMEM((rows // 128, 128), jnp.int32),
            pltpu.VMEM((2, rows, rows), BF),
            *[pltpu.VMEM(((rows + 2 * bnd) // tile, tile, width), BF)] * ORDER,
            pltpu.VMEM((blocks, per_block, tile, tile), BF),
            pltpu.VMEM((2 * bnd, rows), BF),
            pltpu.VMEM((ORDER, 2 * bnd // tile, tile, width), BF),
            pltpu.VMEM((rows, width), F32),
            pltpu.VMEM((rows, width), BF),
            pltpu.VMEM((lanes, rows, width), BF),
            pltpu.VMEM((lanes, rows // 128, 128), jnp.int32),
            pltpu.VMEM((groups, share, width), F32),
            pltpu.VMEM((groups, share, width), F32),
            pltpu.VMEM((lanes, share, width), F32),
            pltpu.VMEM((share, width), F32),
            pltpu.VMEM((groups, share, width), F32),
            pltpu.VMEM((rows, width), BF),
            dma((8,)),
            dma((ORDER, 2)), dma((ORDER, 2)),
            dma((lanes,)), dma((lanes,)),
            dma((groups,)), dma((groups,)),
            dma((lanes,)), dma((lanes,)),
            dma((groups,)), dma((groups,)),
            dma((half,)), dma((half,)),
            dma((half,)), dma((half,)),
        ],
        compiler_params=pltpu.CompilerParams(
            collective_id=0, has_side_effects=True, vmem_limit_bytes=52 * 1024 * 1024
        ),
    )(
        tile_cols, send_count, features.reshape(-1, tile, width), tiles, send_index.reshape(2, bnd), coef,
        dest_lane.reshape(-1, 128), dest_slot.reshape(-1, 128),
    )


def solution(mesh):
    placed = (
        P(("grp", "lane"), None),
        P(("grp", "lane"), None, None, None),
        P(("grp", "lane"), None),
        P(("grp", "lane"), None, None),
        P(("grp", "lane"), None),
        P(),
        P(("grp", "lane")),
        P(("grp", "lane")),
    )
    return jax.shard_map(
        body, mesh=mesh, in_specs=placed, out_specs=P(("grp", "lane"), None), check_vma=False
    )
```
